32 devices in a mesh: slab: 16 (over z, y, x), feat: 2 (over core).
Axes of the slice: x: 2, y: 2, z: 4, core: 2. Of those that a mesh axis runs over, the one named last changes fastest.
Arguments:
- states: float32 [40, 8192], P(None, ('slab', 'feat')), may hold values from -6 to 6
- inputs: float32 [8192], P(('slab', 'feat')), may hold values from -4 to 4
- targets: float32 [40, 8192], P(None, ('slab', 'feat')), may hold values from -4 to 4
Outputs:
- local_operators: float32 [16, 40, 862], P('slab', 'feat')
- scaled_duals: float32 [16, 40, 862], P('slab', 'feat')
- consensus: float32 [40, 862], P('feat')
- residual_history: float32 [2, 2], replicated
The draws below stay inside these ranges and needn't reach their ends.
All inputs are finite; a program needn't handle non-finite values.
Results may differ from the reference program's by a relative error of at most 0.0003.
Values sent between devices are 32-bit elements; how exact they have to be, the bound alone decides.
A program may use at most 64 MiB of HBM per device.

```python
import jax
import jax.numpy as jnp
from jax import lax

R = 40
ITERS = 2
FEATS = 862
SNAPS = 8192
N_SLAB = 16


def joint_draw(key):
    folded = jax.random.fold_in(key, 9031)
    streams = jax.random.split(folded, 10)
    slab_rows = SNAPS // N_SLAB
    slab_scale = jax.random.uniform(streams[0], (N_SLAB,), minval=0.7, maxval=1.4)
    unit_draw = jnp.clip(jax.random.normal(streams[1], (R, N_SLAB, slab_rows)), -4.0, 4.0)
    states = unit_draw * slab_scale[None, :, None]
    forcing = jnp.clip(jax.random.normal(streams[2], (N_SLAB, slab_rows)), -4.0, 4.0)
    root = R ** 0.5
    linear = jax.random.normal(streams[3], (R, R)) / root
    slab_drift = 0.6 * jax.random.normal(streams[4], (N_SLAB, R, R)) / root
    square_map = 0.3 * jax.random.normal(streams[5], (R, R)) / root
    mixed_map = 0.3 * jax.random.normal(streams[6], (R, R)) / root
    input_gain = jax.random.normal(streams[7], (R,))
    offset = jax.random.normal(streams[8], (R,))
    noise_part = 0.3 * jax.random.normal(streams[9], (R, N_SLAB, slab_rows))
    signal = jnp.einsum('ij,jsk->isk', linear, states)
    signal = signal + jnp.einsum('sij,jsk->isk', slab_drift, states)
    signal = signal + jnp.einsum('ij,jsk->isk', square_map, states * states)
    signal = signal + jnp.einsum('ij,jsk->isk', mixed_map, states * jnp.roll(states, 1, axis=0))
    signal = signal + input_gain[:, None, None] * forcing[None] + offset[:, None, None] + noise_part
    targets = 4.0 * jnp.tanh(signal / 4.0)
    return (states.reshape(R, SNAPS), forcing.reshape(SNAPS), targets.reshape(R, SNAPS))


def draw_states(key, part):
    return joint_draw(key)[0].astype(jnp.float32)


def draw_inputs(key, part):
    return joint_draw(key)[1].astype(jnp.float32)


def draw_targets(key, part):
    return joint_draw(key)[2].astype(jnp.float32)


def setup_inputs(seed: int = 0) -> dict:
    streams_of = jax.random.split(jax.random.key(seed), 4)
    return {
        "states": draw_states(jax.random.fold_in(streams_of[3], 71), 0),
        "inputs": draw_inputs(jax.random.fold_in(streams_of[3], 71), 0),
        "targets": draw_targets(jax.random.fold_in(streams_of[3], 71), 0),
    }


penalty = 1.0

def features(states, inputs):
    reduced = states.shape[0]
    blocks = [states]
    for column in range(reduced):
        blocks.append(states[column:column + 1] * states[column:])
    blocks.append(inputs[None, :])
    blocks.append(jnp.ones_like(inputs)[None, :])
    return jnp.concatenate(blocks, 0)

def reference(states, inputs, targets):
    reduced = states.shape[0]
    slab_rows = states.shape[1] // N_SLAB
    slab_states = states.reshape(reduced, N_SLAB, slab_rows).transpose(1, 0, 2)
    slab_targets = targets.reshape(reduced, N_SLAB, slab_rows).transpose(1, 0, 2)
    slab_inputs = inputs.reshape(N_SLAB, slab_rows)

    def local_solve(packed):
        part_states, part_inputs, part_targets, shifted = packed
        design = features(part_states, part_inputs)
        gram_matrix = jnp.dot(design.astype(jnp.float32), design.T.astype(jnp.float32), precision=lax.Precision.HIGHEST, preferred_element_type=jnp.float32) / slab_rows
        cross = jnp.dot(part_targets.astype(jnp.float32), design.T.astype(jnp.float32), precision=lax.Precision.HIGHEST, preferred_element_type=jnp.float32) / slab_rows
        system = gram_matrix + penalty * jnp.eye(design.shape[0], dtype=jnp.float32)
        return jnp.linalg.solve(system, (cross + penalty * shifted).T).T
    width = FEATS
    consensus = jnp.zeros((reduced, width), jnp.float32)
    duals = jnp.zeros((N_SLAB, reduced, width), jnp.float32)
    primal_list = []
    dual_list = []
    operators = duals
    for sweep in range(ITERS):
        operators = lax.map(local_solve, (slab_states, slab_inputs, slab_targets, consensus[None] - duals))
        updated = lax.optimization_barrier(jnp.sum(operators + duals, 0)) / N_SLAB
        duals = duals + operators - updated[None]
        primal_list.append(jnp.sum(jnp.square(operators - updated[None])))
        dual_list.append(N_SLAB * penalty * penalty * jnp.sum(jnp.square(updated - consensus)))
        consensus = updated
    history = jnp.stack([jnp.stack(primal_list), jnp.stack(dual_list)])
    return (operators, duals, consensus, jnp.sqrt(history / (N_SLAB * reduced * width)))
```

```python
import functools

import jax
import jax.numpy as jnp
from jax import lax
from jax.experimental import pallas as pl
from jax.experimental.pallas import tpu as pltpu
from jax.sharding import PartitionSpec as P

penalty = 1.0
NN = (((1,), (0,)), ((), ()))
NT = (((1,), (1,)), ((), ()))


def exact(left, right, dims=NN):
    return lax.dot_general(left, right, dims, precision=lax.Precision.HIGHEST, preferred_element_type=jnp.float32)


def fast(left, right, dims=NN):
    return lax.dot_general(
        left.astype(jnp.bfloat16), right.astype(jnp.bfloat16), dims, preferred_element_type=jnp.float32
    )


def split(value):
    high = value.astype(jnp.bfloat16)
    return high, (value - high.astype(jnp.float32)).astype(jnp.bfloat16)


def triple(left, right):
    lh, ll = split(left)
    rh, rl = split(right)
    return fast(lh, rh) + (fast(lh, rl) + fast(ll, rh))


def eye_mask(size):
    return lax.broadcasted_iota(jnp.int32, (size, size), 0) == lax.broadcasted_iota(jnp.int32, (size, size), 1)


def refined_solve(right_side, system, inverse):
    answer = fast(right_side, inverse)
    for _ in range(3):
        answer = answer + fast(right_side - exact(answer, system), inverse)
    return answer


def invert_by_pivots(source, target):
    size = source.shape[0]
    target[...] = source[...]
    sub = lax.broadcasted_iota(jnp.int32, (size, 1), 0)
    lane = lax.broadcasted_iota(jnp.int32, (1, size), 1)

    def step(k, carry):
        row = target[pl.ds(k, 1), :]
        here = lane == k
        pivot = jnp.sum(jnp.where(here, row, 0.0), axis=1, keepdims=True)
        scaled = jnp.where(here, 1.0, row) / pivot
        whole = target[...]
        column = jnp.sum(jnp.where(here, whole, 0.0), axis=1, keepdims=True)
        column = jnp.where(sub == k, -1.0, column)
        kept = jnp.where(here | (sub == k), 0.0, whole)
        target[...] = kept - column * scaled
        return carry

    lax.fori_loop(0, size, step, 0)


def first_kernel(states, inputs, targets, local, system, inverse, phi, shifted):
    reduced, count = states.shape
    width = local.shape[1]
    row = 0
    phi[0:reduced, :] = states[...]
    row = reduced
    for i in range(reduced):
        phi[row : row + reduced - i, :] = states[i : i + 1, :] * states[i:reduced, :]
        row += reduced - i
    phi[row : row + 1, :] = inputs[...]
    phi[row + 1 : row + 2, :] = jnp.ones((1, count), jnp.float32)

    s = states[...]
    extra = jnp.concatenate([s * s * (0.5**0.5), jnp.broadcast_to(inputs[...], (8, count)) * (8.0**-0.5)], 0)
    inner = exact(s.T, s)
    system[...] = (inner + 0.5 * inner * inner + exact(extra.T, extra) + 1.0) * (1.0 / count)
    diagonal = eye_mask(count)
    a = system[...] + jnp.where(diagonal, penalty, 0.0)
    system[...] = a

    high = jnp.max(jnp.sum(jnp.abs(a), axis=0, keepdims=True)) / penalty
    delta = (high - 1.0) / (high + 1.0)
    alpha = 2.0 / ((1.0 + high) * penalty)
    c = 2.0 / (2.0 - delta * delta)
    inverse[...] = (c * alpha) * (jnp.where(diagonal, 2.0, 0.0) - alpha * a)
    delta = delta * delta / (2.0 - delta * delta)

    def coarse(state):
        step, delta = state
        x = inverse[...].astype(jnp.bfloat16)
        shifted[...] = fast(system[...], x)
        c = 2.0 / (2.0 - delta * delta)
        inverse[...] = c * (2.0 * inverse[...] - fast(x, shifted[...]))
        return step + 1, delta * delta / (2.0 - delta * delta)

    lax.while_loop(lambda state: (state[1] > 0.1) & (state[0] < 12), coarse, (0, delta))

    def polish(state):
        step, _ = state
        x = inverse[...]
        gap = jnp.where(eye_mask(count), 1.0, 0.0) - triple(system[...], x)
        shifted[...] = gap
        worst = jnp.sum(jnp.sum(gap * gap, axis=0, keepdims=True))
        inverse[...] = inverse[...] + fast(inverse[...], shifted[...])
        return step + 1, worst

    _, worst = lax.while_loop(
        lambda state: jnp.logical_not(state[1] < 0.02) & (state[0] < 6), polish, (0, jnp.float32(1e9))
    )

    @pl.when(jnp.logical_not(worst < 0.02))
    def _():
        invert_by_pivots(system, inverse)

    y = refined_solve(targets[...] * (1.0 / count), system[...], inverse[...])
    local[...] = exact(y, phi[...], NT)


def second_step(local, mean, system, inverse, phi):
    c = 2.0 * mean - local
    z = exact(c, phi) * (1.0 / (phi.shape[1] * penalty))
    return 2.0 * mean - exact(refined_solve(z, system, inverse), phi, NT)


def second_kernel(local, mean, system, inverse, phi, out):
    out[...] = second_step(local[...], mean[...], system[...], inverse[...], phi[...])


PARAMS = dict(vmem_limit_bytes=60 * 2**20)


def first_call(states, inputs, targets, width):
    count = states.shape[1]
    vmem = pl.BlockSpec(memory_space=pltpu.VMEM)
    square = jax.ShapeDtypeStruct((count, count), jnp.float32)
    return pl.pallas_call(
        first_kernel,
        out_shape=(
            jax.ShapeDtypeStruct((targets.shape[0], width), jnp.float32),
            square,
            square,
            jax.ShapeDtypeStruct((width, count), jnp.float32),
        ),
        in_specs=[vmem] * 3,
        out_specs=(vmem,) * 4,
        scratch_shapes=[pltpu.VMEM((count, count), jnp.float32)],
        compiler_params=pltpu.CompilerParams(**PARAMS),
        name="local_first",
    )(states, inputs, targets)


def shards(states, inputs, targets):
    reduced = states.shape[0]
    feat_count = lax.axis_size("feat")
    slab_count = lax.axis_size("slab")
    half = reduced // feat_count
    width = reduced + reduced * (reduced + 1) // 2 + 2
    packed = jnp.concatenate([states, targets, inputs[None]], 0)
    full = lax.all_gather(packed, "feat", axis=1, tiled=True)
    first_row = lax.axis_index("feat") * half
    picked = lax.dynamic_slice_in_dim(full[reduced : 2 * reduced], first_row, half, 0)
    local, system, inverse, phi = first_call(full[:reduced], full[2 * reduced :], picked, width)
    mean = lax.psum(local, "slab") / slab_count
    vmem = pl.BlockSpec(memory_space=pltpu.VMEM)
    after = pl.pallas_call(
        second_kernel,
        out_shape=jax.ShapeDtypeStruct(local.shape, jnp.float32),
        in_specs=[vmem] * 5,
        out_specs=vmem,
        compiler_params=pltpu.CompilerParams(**PARAMS),
        name="local_second",
    )(local, mean, system, inverse, phi)
    last = lax.psum(after, "slab") / slab_count
    duals = (local - mean) + (after - last)
    sums = jnp.stack(
        [
            jnp.sum(jnp.square(local - mean)),
            jnp.sum(jnp.square(after - last)),
            penalty * penalty * jnp.sum(jnp.square(mean)),
            penalty * penalty * jnp.sum(jnp.square(last - mean)),
        ]
    )
    history = lax.psum(sums, ("slab", "feat")).reshape(2, 2)
    residual_history = jnp.sqrt(history / (slab_count * reduced * width))
    return (after[None], duals[None], last, residual_history)


def solution(mesh):
    in_specs = (P(None, ("slab", "feat")), P(("slab", "feat")), P(None, ("slab", "feat")))
    out_specs = (P("slab", "feat", None), P("slab", "feat", None), P("feat", None), P())
    return jax.shard_map(shards, mesh=mesh, in_specs=in_specs, out_specs=out_specs, check_vma=False)
```

```python
import functools

import jax
import jax.numpy as jnp
from jax import lax
from jax.experimental import pallas as pl
from jax.experimental.pallas import tpu as pltpu
from jax.sharding import PartitionSpec as P

penalty = 1.0
NN = (((1,), (0,)), ((), ()))
NT = (((1,), (1,)), ((), ()))


def exact(left, right, dims=NN):
    return lax.dot_general(left, right, dims, precision=lax.Precision.HIGHEST, preferred_element_type=jnp.float32)


def fast(left, right, dims=NN):
    return lax.dot_general(
        left.astype(jnp.bfloat16), right.astype(jnp.bfloat16), dims, preferred_element_type=jnp.float32
    )


def split(value):
    high = value.astype(jnp.bfloat16)
    return high, (value - high.astype(jnp.float32)).astype(jnp.bfloat16)


def triple(left, right):
    lh, ll = split(left)
    rh, rl = split(right)
    return fast(lh, rh) + (fast(lh, rl) + fast(ll, rh))


def eye_mask(size):
    return lax.broadcasted_iota(jnp.int32, (size, size), 0) == lax.broadcasted_iota(jnp.int32, (size, size), 1)


def refined_solve(right_side, system, inverse):
    answer = fast(right_side, inverse)
    for _ in range(3):
        answer = answer + fast(right_side - exact(answer, system), inverse)
    return answer


def invert_by_pivots(source, target):
    size = source.shape[0]
    target[...] = source[...]
    sub = lax.broadcasted_iota(jnp.int32, (size, 1), 0)
    lane = lax.broadcasted_iota(jnp.int32, (1, size), 1)

    def step(k, carry):
        row = target[pl.ds(k, 1), :]
        here = lane == k
        pivot = jnp.sum(jnp.where(here, row, 0.0), axis=1, keepdims=True)
        scaled = jnp.where(here, 1.0, row) / pivot
        whole = target[...]
        column = jnp.sum(jnp.where(here, whole, 0.0), axis=1, keepdims=True)
        column = jnp.where(sub == k, -1.0, column)
        kept = jnp.where(here | (sub == k), 0.0, whole)
        target[...] = kept - column * scaled
        return carry

    lax.fori_loop(0, size, step, 0)


def first_kernel(packed, local, tiles, system, inverse, phi, shifted, wanted, *, reduced, feats):
    count = packed.shape[1]
    half = reduced // feats
    row = reduced
    phi[0:reduced, :] = packed[0:reduced, :]
    for i in range(reduced):
        phi[row : row + reduced - i, :] = packed[i : i + 1, :] * packed[i:reduced, :]
        row += reduced - i
    signal = packed[2 * reduced : 2 * reduced + 1, :]
    phi[row : row + 1, :] = signal
    phi[row + 1 : row + 2, :] = jnp.ones((1, count), jnp.float32)
    if row + 2 < phi.shape[0]:
        phi[row + 2 :, :] = jnp.zeros((phi.shape[0] - row - 2, count), jnp.float32)
    wanted[...] = jnp.zeros(wanted.shape, jnp.float32)
    me = lax.axis_index("feat")
    for f in range(feats):

        @pl.when(me == f)
        def _():
            wanted[0:half, :] = packed[reduced + f * half : reduced + (f + 1) * half, :]

    s = packed[0:reduced, :]
    extra = jnp.concatenate([s * s * (0.5**0.5), jnp.broadcast_to(signal, (8, count)) * (8.0**-0.5)], 0)
    inner = exact(s.T, s)
    diagonal = eye_mask(count)
    a = (inner + 0.5 * inner * inner + exact(extra.T, extra) + 1.0) * (1.0 / count)
    a = a + jnp.where(diagonal, penalty, 0.0)
    system[...] = a

    high = jnp.max(jnp.sum(jnp.abs(a), axis=0, keepdims=True)) / penalty
    delta = (high - 1.0) / (high + 1.0)
    alpha = 2.0 / ((1.0 + high) * penalty)
    c = 2.0 / (2.0 - delta * delta)
    inverse[...] = (c * alpha) * (jnp.where(diagonal, 2.0, 0.0) - alpha * a)
    delta = delta * delta / (2.0 - delta * delta)

    def coarse(state):
        step, delta = state
        x = inverse[...].astype(jnp.bfloat16)
        shifted[...] = fast(system[...], x)
        c = 2.0 / (2.0 - delta * delta)
        inverse[...] = c * (2.0 * inverse[...] - fast(x, shifted[...]))
        return step + 1, delta * delta / (2.0 - delta * delta)

    lax.while_loop(lambda state: (state[1] > 0.1) & (state[0] < 12), coarse, (0, delta))

    def polish(state):
        step, _ = state
        x = inverse[...]
        gap = jnp.where(eye_mask(count), 1.0, 0.0) - triple(system[...], x)
        shifted[...] = gap
        worst = jnp.sum(jnp.sum(gap * gap, axis=0, keepdims=True))
        inverse[...] = inverse[...] + fast(inverse[...], shifted[...])
        return step + 1, worst

    _, worst = lax.while_loop(
        lambda state: jnp.logical_not(state[1] < 0.02) & (state[0] < 6), polish, (0, jnp.float32(1e9))
    )

    @pl.when(jnp.logical_not(worst < 0.02))
    def _():
        invert_by_pivots(system, inverse)

    y = refined_solve(wanted[...] * (1.0 / count), system[...], inverse[...])
    result = exact(y, phi[...], NT)
    local[...] = result
    to_tiles(result, tiles)


def to_tiles(value, tiles):
    rows, columns = value.shape
    spot = 0
    for c in range(0, columns, 128):
        for r in range(0, rows, 8):
            tiles[spot] = value[r : r + 8, c : c + 128]
            spot += 1
    for rest in range(spot, tiles.shape[0]):
        tiles[rest] = jnp.zeros((8, 128), jnp.float32)


def from_tiles(tile, rows, columns):
    high = rows // 8
    strips = []
    for c in range(columns // 128):
        strips.append(jnp.concatenate([tile(c * high + r) for r in range(high)], 0))
    return jnp.concatenate(strips, 1)


def total(value):
    flat = value.reshape(-1, 8, 128).sum(0)
    return jnp.sum(jnp.sum(flat, axis=1, keepdims=True), axis=0, keepdims=True)


def second_kernel(
    local, tiles, system, inverse, phi, after, duals, last, history,
    received, gathered, received2, gathered2, foreign, tiles2, stats,
    scatter_send, scatter_recv, gather_send, gather_recv,
    scatter_send2, scatter_recv2, gather_send2, gather_recv2, foreign_send, foreign_recv,
    *, reduced, width,
):
    slabs = lax.axis_size("slab")
    feats = lax.axis_size("feat")
    me = lax.axis_index("slab")
    core = lax.axis_index("feat")
    owners, extended = gathered2.shape[0], gathered2.shape[1]
    chunk = extended - 1
    rows, columns = local.shape
    half = reduced // feats

    def peer(d):
        return lax.rem(me + d, slabs)

    def feat_of(f):
        return lax.rem(core + f, feats)

    def copy(source, target, send, recv, slab, feat):
        return pltpu.make_async_remote_copy(
            src_ref=source, dst_ref=target, send_sem=send, recv_sem=recv,
            device_id={"slab": slab, "feat": feat}, device_id_type=pl.DeviceIdType.MESH,
        )

    barrier = pltpu.get_barrier_semaphore()
    for f in range(feats):

        def greet(d, carry, f=f):
            pl.semaphore_signal(
                barrier, inc=1, device_id={"slab": peer(d), "feat": feat_of(f)},
                device_id_type=pl.DeviceIdType.MESH,
            )
            return carry

        lax.fori_loop(1 if f == 0 else 0, slabs, greet, 0)
    pl.semaphore_wait(barrier, slabs * feats - 1)

    def each(first, stop, body):
        def step(d, carry):
            body(d)
            return carry

        lax.fori_loop(first, stop, step, 0)

    def scatter(source, landing, send, recv):
        def piece(d):
            owner = peer(d)
            return copy(source.at[pl.ds(owner * chunk, chunk)], landing.at[d], send.at[d], recv.at[d], owner, core)

        def start(d):
            @pl.when(peer(d) < owners)
            def _():
                piece(d).start()

        def finish(d):
            @pl.when(peer(d) < owners)
            def _():
                piece(d).wait_send()

        each(1, slabs, start)
        return finish

    def arrivals(source, landing, send, recv):
        def wait(d):
            copy(source.at[pl.ds(0, chunk)], landing.at[d], send.at[d], recv.at[d], me, core).wait_recv()

        each(1, slabs, wait)

    def spread(buffer, send, recv):
        def piece(d):
            return copy(buffer.at[me], buffer.at[me], send.at[d], recv.at[me], peer(d), core)

        each(1, slabs, lambda d: piece(d).start())
        return lambda d: piece(d).wait_send()

    def collected(buffer, send, recv):
        def wait(o):
            @pl.when(o != me)
            def _():
                copy(buffer.at[o], buffer.at[o], send.at[0], recv.at[o], me, core).wait_recv()

        each(0, owners, wait)

    end1 = scatter(tiles, received, scatter_send, scatter_recv)

    @pl.when(me < owners)
    def _():
        arrivals(tiles, received, scatter_send, scatter_recv)
        mine = tiles[pl.ds(me * chunk, chunk)]
        others = received[1:slabs]
        mean = (mine + others.sum(0)) * (1.0 / slabs)
        gathered[me] = mean
        spread(gathered, gather_send, gather_recv)
        primal = total(jnp.square(mine - mean)) + total(jnp.square(others - mean[None]))
        stats[0] = jnp.broadcast_to(primal, (8, 128))
        stats[1] = jnp.broadcast_to((slabs * penalty * penalty) * total(jnp.square(mean)), (8, 128))

    collected(gathered, gather_send, gather_recv)
    mean = from_tiles(lambda t: gathered[t // chunk, t % chunk], rows, columns)
    first = local[...]
    c = 2.0 * mean - first
    z = exact(c, phi[...]) * (1.0 / (phi.shape[1] * penalty))
    result = 2.0 * mean - exact(refined_solve(z, system[...], inverse[...]), phi[...], NT)
    to_tiles(result, tiles2)
    end2 = scatter(tiles2, received2, scatter_send2, scatter_recv2)
    after[...] = result[:half, :width]

    @pl.when(me < owners)
    def _():
        arrivals(tiles2, received2, scatter_send2, scatter_recv2)
        mine = tiles2[pl.ds(me * chunk, chunk)]
        others = received2[1:slabs]
        old = gathered[me]
        new = (mine + others.sum(0)) * (1.0 / slabs)
        primal = total(jnp.square(mine - new)) + total(jnp.square(others - new[None]))
        dual = (slabs * penalty * penalty) * total(jnp.square(new - old))
        sub = lax.broadcasted_iota(jnp.int32, (8, 128), 0)
        lane = lax.broadcasted_iota(jnp.int32, (8, 128), 1)
        top = jnp.where(lane == 0, stats[0], jnp.broadcast_to(primal, (8, 128)))
        low = jnp.where(lane == 0, stats[1], jnp.broadcast_to(dual, (8, 128)))
        gathered2[me, 0:chunk] = new
        gathered2[me, chunk] = jnp.where(sub == 0, top, low)
        spread(gathered2, gather_send2, gather_recv2)
        for f in range(1, feats):

            def outward(d, f=f):
                copy(
                    gathered2.at[me, chunk], foreign.at[f - 1, me], foreign_send.at[f - 1, d],
                    foreign_recv.at[f - 1, me], peer(d), feat_of(f),
                ).start()

            each(0, slabs, outward)

    collected(gathered2, gather_send2, gather_recv2)
    new = from_tiles(lambda t: gathered2[t // chunk, t % chunk], rows, columns)
    last[...] = new[:half, :width]
    change = (first - mean) + (result - new)
    duals[...] = change[:half, :width]
    sums = gathered2[0, chunk]
    for o in range(1, owners):
        sums = sums + gathered2[o, chunk]
    for f in range(1, feats):

        def inward(o, f=f):
            copy(
                gathered2.at[0, chunk], foreign.at[f - 1, o], foreign_send.at[f - 1, 0],
                foreign_recv.at[f - 1, o], me, core,
            ).wait_recv()

        each(0, owners, inward)
        for o in range(owners):
            sums = sums + foreign[f - 1, o]
    history[...] = jnp.sqrt(sums * (1.0 / (slabs * reduced * width)))[0:2, 0:2]

    each(1, slabs, end1)
    each(1, slabs, end2)

    @pl.when(me < owners)
    def _():
        def leave(d):
            copy(gathered.at[me], gathered.at[me], gather_send.at[d], gather_recv.at[me], peer(d), core).wait_send()
            copy(
                gathered2.at[me], gathered2.at[me], gather_send2.at[d], gather_recv2.at[me], peer(d), core
            ).wait_send()

        each(1, slabs, leave)
        for f in range(1, feats):

            def depart(d, f=f):
                copy(
                    gathered2.at[me, chunk], foreign.at[f - 1, me], foreign_send.at[f - 1, d],
                    foreign_recv.at[f - 1, me], peer(d), feat_of(f),
                ).wait_send()

            each(0, slabs, depart)


LIMIT = 60 * 2**20


def up(value, step):
    return -(-value // step) * step


def shards(states, inputs, targets):
    reduced = states.shape[0]
    feats = lax.axis_size("feat")
    slabs = lax.axis_size("slab")
    half = reduced // feats
    width = reduced + reduced * (reduced + 1) // 2 + 2
    count = states.shape[1] * feats
    rows, columns = up(half, 8), up(width, 128)
    pieces = (rows // 8) * (columns // 128)
    chunk = -(-pieces // slabs)
    owners = -(-pieces // chunk)
    f32 = jnp.float32
    packed = lax.all_gather(jnp.concatenate([states, targets, inputs[None]], 0), "feat", axis=1, tiled=True)
    vmem = pl.BlockSpec(memory_space=pltpu.VMEM)
    square = jax.ShapeDtypeStruct((count, count), f32)
    local, tiles, system, inverse, phi = pl.pallas_call(
        functools.partial(first_kernel, reduced=reduced, feats=feats),
        out_shape=(
            jax.ShapeDtypeStruct((rows, columns), f32),
            jax.ShapeDtypeStruct((owners * chunk, 8, 128), f32),
            square,
            square,
            jax.ShapeDtypeStruct((columns, count), f32),
        ),
        in_specs=[vmem],
        out_specs=(vmem,) * 5,
        scratch_shapes=[pltpu.VMEM((count, count), f32), pltpu.VMEM((rows, count), f32)],
        compiler_params=pltpu.CompilerParams(vmem_limit_bytes=LIMIT),
        name="local_first",
    )(packed)
    shard = jax.ShapeDtypeStruct((half, width), f32)
    dma = pltpu.SemaphoreType.DMA
    after, duals, last, history = pl.pallas_call(
        functools.partial(second_kernel, reduced=reduced, width=width),
        out_shape=(shard, shard, shard, jax.ShapeDtypeStruct((2, 2), f32)),
        in_specs=[vmem] * 5,
        out_specs=(vmem,) * 4,
        scratch_shapes=[
            pltpu.VMEM((slabs, chunk, 8, 128), f32),
            pltpu.VMEM((owners, chunk, 8, 128), f32),
            pltpu.VMEM((slabs, chunk, 8, 128), f32),
            pltpu.VMEM((owners, chunk + 1, 8, 128), f32),
            pltpu.VMEM((max(feats - 1, 1), owners, 8, 128), f32),
            pltpu.VMEM((owners * chunk, 8, 128), f32),
            pltpu.VMEM((2, 8, 128), f32),
            dma((slabs,)), dma((slabs,)), dma((slabs,)), dma((owners,)),
            dma((slabs,)), dma((slabs,)), dma((slabs,)), dma((owners,)),
            dma((max(feats - 1, 1), slabs)), dma((max(feats - 1, 1), owners)),
        ],
        compiler_params=pltpu.CompilerParams(vmem_limit_bytes=LIMIT, collective_id=0, has_side_effects=True),
        name="second_and_averages",
    )(local, tiles, system, inverse, phi)
    return (after[None], duals[None], last, history)


def solution(mesh):
    in_specs = (P(None, ("slab", "feat")), P(("slab", "feat")), P(None, ("slab", "feat")))
    out_specs = (P("slab", "feat", None), P("slab", "feat", None), P("feat", None), P())
    return jax.shard_map(shards, mesh=mesh, in_specs=in_specs, out_specs=out_specs, check_vma=False)
```

```python
import functools

import jax
import jax.numpy as jnp
from jax import lax
from jax.experimental import pallas as pl
from jax.experimental.pallas import tpu as pltpu
from jax.sharding import PartitionSpec as P

penalty = 1.0
NN = (((1,), (0,)), ((), ()))
NT = (((1,), (1,)), ((), ()))


def exact(left, right, dims=NN):
    return lax.dot_general(left, right, dims, precision=lax.Precision.HIGHEST, preferred_element_type=jnp.float32)


def fast(left, right, dims=NN):
    return lax.dot_general(
        left.astype(jnp.bfloat16), right.astype(jnp.bfloat16), dims, preferred_element_type=jnp.float32
    )


def split(value):
    high = value.astype(jnp.bfloat16)
    return high, (value - high.astype(jnp.float32)).astype(jnp.bfloat16)


def triple(left, right):
    lh, ll = split(left)
    rh, rl = split(right)
    return fast(lh, rh) + (fast(lh, rl) + fast(ll, rh))


def eye_mask(size):
    return lax.broadcasted_iota(jnp.int32, (size, size), 0) == lax.broadcasted_iota(jnp.int32, (size, size), 1)


def refined_solve(right_side, system, inverse):
    answer = fast(right_side, inverse)
    for _ in range(3):
        answer = answer + fast(right_side - exact(answer, system), inverse)
    return answer


def invert_by_pivots(source, target):
    size = source.shape[0]
    target[...] = source[...]
    sub = lax.broadcasted_iota(jnp.int32, (size, 1), 0)
    lane = lax.broadcasted_iota(jnp.int32, (1, size), 1)

    def step(k, carry):
        row = target[pl.ds(k, 1), :]
        here = lane == k
        pivot = jnp.sum(jnp.where(here, row, 0.0), axis=1, keepdims=True)
        scaled = jnp.where(here, 1.0, row) / pivot
        whole = target[...]
        column = jnp.sum(jnp.where(here, whole, 0.0), axis=1, keepdims=True)
        column = jnp.where(sub == k, -1.0, column)
        kept = jnp.where(here | (sub == k), 0.0, whole)
        target[...] = kept - column * scaled
        return carry

    lax.fori_loop(0, size, step, 0)


def first_kernel(packed, local, tiles, system, inverse, phi, shifted, wanted, *, reduced, feats):
    count = packed.shape[1]
    half = reduced // feats
    row = reduced
    phi[0:reduced, :] = packed[0:reduced, :]
    for i in range(reduced):
        phi[row : row + reduced - i, :] = packed[i : i + 1, :] * packed[i:reduced, :]
        row += reduced - i
    signal = packed[2 * reduced : 2 * reduced + 1, :]
    phi[row : row + 1, :] = signal
    phi[row + 1 : row + 2, :] = jnp.ones((1, count), jnp.float32)
    if row + 2 < phi.shape[0]:
        phi[row + 2 :, :] = jnp.zeros((phi.shape[0] - row - 2, count), jnp.float32)
    wanted[...] = jnp.zeros(wanted.shape, jnp.float32)
    me = lax.axis_index("feat")
    for f in range(feats):

        @pl.when(me == f)
        def _():
            wanted[0:half, :] = packed[reduced + f * half : reduced + (f + 1) * half, :]

    s = packed[0:reduced, :]
    extra = jnp.concatenate([s * s * (0.5**0.5), jnp.broadcast_to(signal, (8, count)) * (8.0**-0.5)], 0)
    inner = exact(s.T, s)
    diagonal = eye_mask(count)
    a = (inner + 0.5 * inner * inner + exact(extra.T, extra) + 1.0) * (1.0 / count)
    a = a + jnp.where(diagonal, penalty, 0.0)
    system[...] = a

    high = jnp.max(jnp.sum(jnp.abs(a), axis=0, keepdims=True)) / penalty
    delta = (high - 1.0) / (high + 1.0)
    alpha = 2.0 / ((1.0 + high) * penalty)
    c = 2.0 / (2.0 - delta * delta)
    inverse[...] = (c * alpha) * (jnp.where(diagonal, 2.0, 0.0) - alpha * a)
    delta = delta * delta / (2.0 - delta * delta)

    def coarse(state):
        step, delta = state
        x = inverse[...].astype(jnp.bfloat16)
        shifted[...] = fast(system[...], x)
        c = 2.0 / (2.0 - delta * delta)
        inverse[...] = c * (2.0 * inverse[...] - fast(x, shifted[...]))
        return step + 1, delta * delta / (2.0 - delta * delta)

    lax.while_loop(lambda state: (state[1] > 0.1) & (state[0] < 12), coarse, (0, delta))

    def polish(state):
        step, _ = state
        x = inverse[...]
        gap = jnp.where(eye_mask(count), 1.0, 0.0) - triple(system[...], x)
        shifted[...] = gap
        worst = jnp.sum(jnp.sum(gap * gap, axis=0, keepdims=True))
        inverse[...] = inverse[...] + fast(inverse[...], shifted[...])
        return step + 1, worst

    _, worst = lax.while_loop(
        lambda state: jnp.logical_not(state[1] < 0.02) & (state[0] < 6), polish, (0, jnp.float32(1e9))
    )

    @pl.when(jnp.logical_not(worst < 0.02))
    def _():
        invert_by_pivots(system, inverse)

    y = refined_solve(wanted[...] * (1.0 / count), system[...], inverse[...])
    result = exact(y, phi[...], NT)
    local[...] = result
    to_tiles(result, tiles)


def to_tiles(value, tiles):
    rows, columns = value.shape
    spot = 0
    for c in range(0, columns, 128):
        for r in range(0, rows, 8):
            tiles[spot] = value[r : r + 8, c : c + 128]
            spot += 1
    for rest in range(spot, tiles.shape[0]):
        tiles[rest] = jnp.zeros((8, 128), jnp.float32)


def from_tiles(tile, rows, columns):
    high = rows // 8
    strips = []
    for c in range(columns // 128):
        strips.append(jnp.concatenate([tile(c * high + r) for r in range(high)], 0))
    return jnp.concatenate(strips, 1)


def total(value):
    flat = value.reshape(-1, 8, 128).sum(0)
    return jnp.sum(jnp.sum(flat, axis=1, keepdims=True), axis=0, keepdims=True)


def second_kernel(
    local, tiles, system, inverse, phi, after, duals, last, history,
    received, gathered, received2, gathered2, foreign, tiles2, stats,
    scatter_send, scatter_recv, gather_send, gather_recv,
    scatter_send2, scatter_recv2, gather_send2, gather_recv2, foreign_send, foreign_recv,
    *, reduced, width,
):
    slabs = lax.axis_size("slab")
    feats = lax.axis_size("feat")
    me = lax.axis_index("slab")
    core = lax.axis_index("feat")
    owners, extended = gathered2.shape[0], gathered2.shape[1]
    chunk = extended - 1
    rows, columns = local.shape

    def peer(d):
        return lax.rem(me + d, slabs)

    def feat_of(f):
        return lax.rem(core + f, feats)

    def copy(source, target, send, recv, slab, feat):
        return pltpu.make_async_remote_copy(
            src_ref=source, dst_ref=target, send_sem=send, recv_sem=recv,
            device_id={"slab": slab, "feat": feat}, device_id_type=pl.DeviceIdType.MESH,
        )

    def each(first, stop, body):
        if stop - first <= 16:
            for d in range(first, stop):
                body(d)
            return

        def step(d, carry):
            body(d)
            return carry

        lax.fori_loop(first, stop, step, 0)

    barrier = pltpu.get_barrier_semaphore()
    for f in range(feats):

        def greet(d, f=f):
            pl.semaphore_signal(
                barrier, inc=1, device_id={"slab": peer(d), "feat": feat_of(f)},
                device_id_type=pl.DeviceIdType.MESH,
            )

        each(1 if f == 0 else 0, slabs, greet)
    pl.semaphore_wait(barrier, slabs * feats - 1)

    def scatter(source, landing, send, recv):
        def piece(d):
            owner = peer(d)
            return copy(source.at[pl.ds(owner * chunk, chunk)], landing.at[d], send.at[d], recv.at[d], owner, core)

        def start(d):
            @pl.when(peer(d) < owners)
            def _():
                piece(d).start()

        def finish(d):
            @pl.when(peer(d) < owners)
            def _():
                piece(d).wait_send()

        each(1, slabs, start)
        return finish

    def arrivals(source, landing, send, recv):
        def wait(d):
            copy(source.at[pl.ds(0, chunk)], landing.at[d], send.at[d], recv.at[d], me, core).wait_recv()

        each(1, slabs, wait)

    def spread(buffer, send, recv):
        def piece(d):
            return copy(buffer.at[me], buffer.at[me], send.at[d], recv.at[me], peer(d), core)

        each(1, slabs, lambda d: piece(d).start())
        return lambda d: piece(d).wait_send()

    def collected(buffer, send, recv):
        def wait(o):
            @pl.when(o != me)
            def _():
                copy(buffer.at[o], buffer.at[o], send.at[0], recv.at[o], me, core).wait_recv()

        each(0, owners, wait)

    end1 = scatter(tiles, received, scatter_send, scatter_recv)

    @pl.when(me < owners)
    def _():
        arrivals(tiles, received, scatter_send, scatter_recv)
        mine = tiles[pl.ds(me * chunk, chunk)]
        others = received[1:slabs]
        mean = (mine + others.sum(0)) * (1.0 / slabs)
        gathered[me] = mean
        spread(gathered, gather_send, gather_recv)
        primal = total(jnp.square(mine - mean)) + total(jnp.square(others - mean[None]))
        stats[0] = jnp.broadcast_to(primal, (8, 128))
        stats[1] = jnp.broadcast_to((slabs * penalty * penalty) * total(jnp.square(mean)), (8, 128))

    collected(gathered, gather_send, gather_recv)
    mean = from_tiles(lambda t: gathered[t // chunk, t % chunk], rows, columns)
    first = local[...]
    c = 2.0 * mean - first
    z = exact(c, phi[...]) * (1.0 / (phi.shape[1] * penalty))
    result = 2.0 * mean - exact(refined_solve(z, system[...], inverse[...]), phi[...], NT)
    to_tiles(result, tiles2)
    end2 = scatter(tiles2, received2, scatter_send2, scatter_recv2)
    after[...] = result

    @pl.when(me < owners)
    def _():
        arrivals(tiles2, received2, scatter_send2, scatter_recv2)
        mine = tiles2[pl.ds(me * chunk, chunk)]
        others = received2[1:slabs]
        old = gathered[me]
        new = (mine + others.sum(0)) * (1.0 / slabs)
        primal = total(jnp.square(mine - new)) + total(jnp.square(others - new[None]))
        dual = (slabs * penalty * penalty) * total(jnp.square(new - old))
        sub = lax.broadcasted_iota(jnp.int32, (8, 128), 0)
        lane = lax.broadcasted_iota(jnp.int32, (8, 128), 1)
        top = jnp.where(lane == 0, stats[0], jnp.broadcast_to(primal, (8, 128)))
        low = jnp.where(lane == 0, stats[1], jnp.broadcast_to(dual, (8, 128)))
        gathered2[me, 0:chunk] = new
        gathered2[me, chunk] = jnp.where(sub == 0, top, low)
        spread(gathered2, gather_send2, gather_recv2)
        for f in range(1, feats):

            def outward(d, f=f):
                copy(
                    gathered2.at[me, chunk], foreign.at[f - 1, me], foreign_send.at[f - 1, d],
                    foreign_recv.at[f - 1, me], peer(d), feat_of(f),
                ).start()

            each(0, slabs, outward)

    collected(gathered2, gather_send2, gather_recv2)
    new = from_tiles(lambda t: gathered2[t // chunk, t % chunk], rows, columns)
    last[...] = new
    change = (first - mean) + (result - new)
    duals[...] = change
    sums = gathered2[0, chunk]
    for o in range(1, owners):
        sums = sums + gathered2[o, chunk]
    for f in range(1, feats):

        def inward(o, f=f):
            copy(
                gathered2.at[0, chunk], foreign.at[f - 1, o], foreign_send.at[f - 1, 0],
                foreign_recv.at[f - 1, o], me, core,
            ).wait_recv()

        each(0, owners, inward)
        for o in range(owners):
            sums = sums + foreign[f - 1, o]
    history[...] = jnp.sqrt(sums * (1.0 / (slabs * reduced * width)))

    each(1, slabs, end1)
    each(1, slabs, end2)

    @pl.when(me < owners)
    def _():
        def leave(d):
            copy(gathered.at[me], gathered.at[me], gather_send.at[d], gather_recv.at[me], peer(d), core).wait_send()
            copy(
                gathered2.at[me], gathered2.at[me], gather_send2.at[d], gather_recv2.at[me], peer(d), core
            ).wait_send()

        each(1, slabs, leave)
        for f in range(1, feats):

            def depart(d, f=f):
                copy(
                    gathered2.at[me, chunk], foreign.at[f - 1, me], foreign_send.at[f - 1, d],
                    foreign_recv.at[f - 1, me], peer(d), feat_of(f),
                ).wait_send()

            each(0, slabs, depart)


def last_kernel(after, duals, last, history, out_after, out_duals, out_last, out_history):
    half, width = out_last.shape
    for r in range(half):
        out_after[r] = after[r : r + 1, :width]
        out_duals[r] = duals[r : r + 1, :width]
    out_last[...] = last[:half, :width]
    out_history[...] = history[0:2, 0:2]


LIMIT = 20 * 2**20


def up(value, step):
    return -(-value // step) * step


def shards(states, inputs, targets):
    reduced = states.shape[0]
    feats = lax.axis_size("feat")
    slabs = lax.axis_size("slab")
    half = reduced // feats
    width = reduced + reduced * (reduced + 1) // 2 + 2
    count = states.shape[1] * feats
    rows, columns = up(half, 8), up(width, 128)
    pieces = (rows // 8) * (columns // 128)
    chunk = -(-pieces // slabs)
    owners = -(-pieces // chunk)
    f32 = jnp.float32
    packed = lax.all_gather(jnp.concatenate([states, targets, inputs[None]], 0), "feat", axis=1, tiled=True)
    vmem = pl.BlockSpec(memory_space=pltpu.VMEM)
    square = jax.ShapeDtypeStruct((count, count), f32)
    local, tiles, system, inverse, phi = pl.pallas_call(
        functools.partial(first_kernel, reduced=reduced, feats=feats),
        out_shape=(
            jax.ShapeDtypeStruct((rows, columns), f32),
            jax.ShapeDtypeStruct((owners * chunk, 8, 128), f32),
            square,
            square,
            jax.ShapeDtypeStruct((columns, count), f32),
        ),
        in_specs=[vmem],
        out_specs=(vmem,) * 5,
        scratch_shapes=[pltpu.VMEM((count, count), f32), pltpu.VMEM((rows, count), f32)],
        compiler_params=pltpu.CompilerParams(vmem_limit_bytes=LIMIT),
        name="local_first",
    )(packed)
    shard = jax.ShapeDtypeStruct((half, width), f32)
    spread_rows = jax.ShapeDtypeStruct((half, 1, width), f32)
    block = jax.ShapeDtypeStruct((rows, columns), f32)
    dma = pltpu.SemaphoreType.DMA
    after, duals, last, history = pl.pallas_call(
        functools.partial(second_kernel, reduced=reduced, width=width),
        out_shape=(block, block, block, jax.ShapeDtypeStruct((8, 128), f32)),
        in_specs=[vmem] * 5,
        out_specs=(vmem,) * 4,
        scratch_shapes=[
            pltpu.VMEM((slabs, chunk, 8, 128), f32),
            pltpu.VMEM((owners, chunk, 8, 128), f32),
            pltpu.VMEM((slabs, chunk, 8, 128), f32),
            pltpu.VMEM((owners, chunk + 1, 8, 128), f32),
            pltpu.VMEM((max(feats - 1, 1), owners, 8, 128), f32),
            pltpu.VMEM((owners * chunk, 8, 128), f32),
            pltpu.VMEM((2, 8, 128), f32),
            dma((slabs,)), dma((slabs,)), dma((slabs,)), dma((owners,)),
            dma((slabs,)), dma((slabs,)), dma((slabs,)), dma((owners,)),
            dma((max(feats - 1, 1), slabs)), dma((max(feats - 1, 1), owners)),
        ],
        compiler_params=pltpu.CompilerParams(vmem_limit_bytes=LIMIT, collective_id=0, has_side_effects=True),
        name="second_and_averages",
    )(local, tiles, system, inverse, phi)
    after, duals, last, history = pl.pallas_call(
        last_kernel,
        out_shape=(spread_rows, spread_rows, shard, jax.ShapeDtypeStruct((2, 2), f32)),
        in_specs=[vmem] * 4,
        out_specs=(vmem,) * 4,
        compiler_params=pltpu.CompilerParams(vmem_limit_bytes=4 * 2**20),
        name="outputs",
    )(after, duals, last, history)
    return (jnp.swapaxes(after, 0, 1), jnp.swapaxes(duals, 0, 1), last, history)


def solution(mesh):
    in_specs = (P(None, ("slab", "feat")), P(("slab", "feat")), P(None, ("slab", "feat")))
    out_specs = (P("slab", "feat", None), P("slab", "feat", None), P("feat", None), P())
    return jax.shard_map(shards, mesh=mesh, in_specs=in_specs, out_specs=out_specs, check_vma=False)
```

```python
import functools

import jax
import jax.numpy as jnp
from jax import lax
from jax.experimental import pallas as pl
from jax.experimental.pallas import tpu as pltpu
from jax.sharding import PartitionSpec as P

penalty = 1.0
NN = (((1,), (0,)), ((), ()))
NT = (((1,), (1,)), ((), ()))


def exact(left, right, dims=NN):
    return lax.dot_general(left, right, dims, precision=lax.Precision.HIGHEST, preferred_element_type=jnp.float32)


def fast(left, right, dims=NN):
    return lax.dot_general(
        left.astype(jnp.bfloat16), right.astype(jnp.bfloat16), dims, preferred_element_type=jnp.float32
    )


def split(value):
    high = value.astype(jnp.bfloat16)
    return high, (value - high.astype(jnp.float32)).astype(jnp.bfloat16)


def triple(left, right):
    lh, ll = split(left)
    rh, rl = split(right)
    return fast(lh, rh) + (fast(lh, rl) + fast(ll, rh))


def eye_mask(size):
    return lax.broadcasted_iota(jnp.int32, (size, size), 0) == lax.broadcasted_iota(jnp.int32, (size, size), 1)


def refined_solve(right_side, system, inverse):
    answer = fast(right_side, inverse)
    for _ in range(3):
        answer = answer + fast(right_side - exact(answer, system), inverse)
    return answer


def invert_by_pivots(source, target):
    size = source.shape[0]
    target[...] = source[...]
    sub = lax.broadcasted_iota(jnp.int32, (size, 1), 0)
    lane = lax.broadcasted_iota(jnp.int32, (1, size), 1)

    def step(k, carry):
        row = target[pl.ds(k, 1), :]
        here = lane == k
        pivot = jnp.sum(jnp.where(here, row, 0.0), axis=1, keepdims=True)
        scaled = jnp.where(here, 1.0, row) / pivot
        whole = target[...]
        column = jnp.sum(jnp.where(here, whole, 0.0), axis=1, keepdims=True)
        column = jnp.where(sub == k, -1.0, column)
        kept = jnp.where(here | (sub == k), 0.0, whole)
        target[...] = kept - column * scaled
        return carry

    lax.fori_loop(0, size, step, 0)


def build_features(packed, phi, wanted, reduced, feats):
    count = packed.shape[1]
    half = reduced // feats
    row = reduced
    phi[0:reduced, :] = packed[0:reduced, :]
    for i in range(reduced):
        phi[row : row + reduced - i, :] = packed[i : i + 1, :] * packed[i:reduced, :]
        row += reduced - i
    phi[row : row + 1, :] = packed[2 * reduced : 2 * reduced + 1, :]
    phi[row + 1 : row + 2, :] = jnp.ones((1, count), jnp.float32)
    if row + 2 < phi.shape[0]:
        phi[row + 2 :, :] = jnp.zeros((phi.shape[0] - row - 2, count), jnp.float32)
    wanted[...] = jnp.zeros(wanted.shape, jnp.float32)
    me = lax.axis_index("feat")
    for f in range(feats):

        @pl.when(me == f)
        def _():
            wanted[0:half, :] = packed[reduced + f * half : reduced + (f + 1) * half, :]


def first_kernel(packed, system, inverse, shifted, *, reduced):
    count = packed.shape[1]
    signal = packed[2 * reduced : 2 * reduced + 1, :]
    s = packed[0:reduced, :]
    extra = jnp.concatenate([s * s * (0.5**0.5), jnp.broadcast_to(signal, (8, count)) * (8.0**-0.5)], 0)
    inner = exact(s.T, s)
    diagonal = eye_mask(count)
    a = (inner + 0.5 * inner * inner + exact(extra.T, extra) + 1.0) * (1.0 / count)
    a = a + jnp.where(diagonal, penalty, 0.0)
    system[...] = a

    high = jnp.max(jnp.sum(jnp.abs(a), axis=0, keepdims=True)) / penalty
    delta = (high - 1.0) / (high + 1.0)
    alpha = 2.0 / ((1.0 + high) * penalty)
    c = 2.0 / (2.0 - delta * delta)
    inverse[...] = (c * alpha) * (jnp.where(diagonal, 2.0, 0.0) - alpha * a)
    delta = delta * delta / (2.0 - delta * delta)

    def coarse(state):
        step, delta = state
        x = inverse[...].astype(jnp.bfloat16)
        shifted[...] = fast(system[...], x)
        c = 2.0 / (2.0 - delta * delta)
        inverse[...] = c * (2.0 * inverse[...] - fast(x, shifted[...]))
        return step + 1, delta * delta / (2.0 - delta * delta)

    lax.while_loop(lambda state: (state[1] > 0.1) & (state[0] < 12), coarse, (0, delta))

    def polish(state):
        step, _ = state
        x = inverse[...]
        gap = jnp.where(eye_mask(count), 1.0, 0.0) - triple(system[...], x)
        shifted[...] = gap
        worst = jnp.sum(jnp.sum(gap * gap, axis=0, keepdims=True))
        inverse[...] = inverse[...] + fast(inverse[...], shifted[...])
        return step + 1, worst

    _, worst = lax.while_loop(
        lambda state: jnp.logical_not(state[1] < 0.02) & (state[0] < 6), polish, (0, jnp.float32(1e9))
    )

    @pl.when(jnp.logical_not(worst < 0.02))
    def _():
        invert_by_pivots(system, inverse)


def to_tiles(value, tiles):
    rows, columns = value.shape
    spot = 0
    for c in range(0, columns, 128):
        for r in range(0, rows, 8):
            tiles[spot] = value[r : r + 8, c : c + 128]
            spot += 1
    for rest in range(spot, tiles.shape[0]):
        tiles[rest] = jnp.zeros((8, 128), jnp.float32)


def from_tiles(tile, rows, columns):
    high = rows // 8
    strips = []
    for c in range(columns // 128):
        strips.append(jnp.concatenate([tile(c * high + r) for r in range(high)], 0))
    return jnp.concatenate(strips, 1)


def total(value):
    flat = value.reshape(-1, 8, 128).sum(0)
    return jnp.sum(jnp.sum(flat, axis=1, keepdims=True), axis=0, keepdims=True)


def second_kernel(
    packed, system, inverse, after, duals, last, history,
    local, tiles, phi, wanted, better, received, gathered, received2, gathered2, foreign, tiles2, stats,
    scatter_send, scatter_recv, gather_send, gather_recv,
    scatter_send2, scatter_recv2, gather_send2, gather_recv2, foreign_send, foreign_recv,
    *, reduced, width,
):
    slabs = lax.axis_size("slab")
    feats = lax.axis_size("feat")
    me = lax.axis_index("slab")
    core = lax.axis_index("feat")
    owners, extended = gathered2.shape[0], gathered2.shape[1]
    chunk = extended - 1
    rows, columns = local.shape

    def peer(d):
        return lax.rem(me + d, slabs)

    def feat_of(f):
        return lax.rem(core + f, feats)

    def copy(source, target, send, recv, slab, feat):
        return pltpu.make_async_remote_copy(
            src_ref=source, dst_ref=target, send_sem=send, recv_sem=recv,
            device_id={"slab": slab, "feat": feat}, device_id_type=pl.DeviceIdType.MESH,
        )

    def each(first, stop, body):
        if stop - first <= 16:
            for d in range(first, stop):
                body(d)
            return

        def step(d, carry):
            body(d)
            return carry

        lax.fori_loop(first, stop, step, 0)

    barrier = pltpu.get_barrier_semaphore()
    for f in range(feats):

        def greet(d, f=f):
            pl.semaphore_signal(
                barrier, inc=1, device_id={"slab": peer(d), "feat": feat_of(f)},
                device_id_type=pl.DeviceIdType.MESH,
            )

        each(1 if f == 0 else 0, slabs, greet)
    build_features(packed, phi, wanted, reduced, feats)
    y = refined_solve(wanted[...] * (1.0 / phi.shape[1]), system[...], inverse[...])
    start_value = exact(y, phi[...], NT)
    local[...] = start_value
    to_tiles(start_value, tiles)
    pl.semaphore_wait(barrier, slabs * feats - 1)

    def scatter(source, landing, send, recv):
        def piece(d):
            owner = peer(d)
            return copy(source.at[pl.ds(owner * chunk, chunk)], landing.at[d], send.at[d], recv.at[d], owner, core)

        def start(d):
            @pl.when(peer(d) < owners)
            def _():
                piece(d).start()

        def finish(d):
            @pl.when(peer(d) < owners)
            def _():
                piece(d).wait_send()

        each(1, slabs, start)
        return finish

    def arrivals(source, landing, send, recv):
        def wait(d):
            copy(source.at[pl.ds(0, chunk)], landing.at[d], send.at[d], recv.at[d], me, core).wait_recv()

        each(1, slabs, wait)

    def spread(buffer, send, recv):
        def piece(d):
            return copy(buffer.at[me], buffer.at[me], send.at[d], recv.at[me], peer(d), core)

        each(1, slabs, lambda d: piece(d).start())
        return lambda d: piece(d).wait_send()

    def collected(buffer, send, recv):
        def wait(o):
            @pl.when(o != me)
            def _():
                copy(buffer.at[o], buffer.at[o], send.at[0], recv.at[o], me, core).wait_recv()

        each(0, owners, wait)

    def polished(x):
        gap = jnp.where(eye_mask(x.shape[0]), 1.0, 0.0) - exact(system[...], x)
        return x + fast(x, gap)

    end1 = scatter(tiles, received, scatter_send, scatter_recv)
    better[...] = polished(inverse[...])

    @pl.when(me < owners)
    def _():
        arrivals(tiles, received, scatter_send, scatter_recv)
        mine = tiles[pl.ds(me * chunk, chunk)]
        others = received[1:slabs]
        mean = (mine + others.sum(0)) * (1.0 / slabs)
        gathered[me] = mean
        spread(gathered, gather_send, gather_recv)
        primal = total(jnp.square(mine - mean)) + total(jnp.square(others - mean[None]))
        stats[0] = jnp.broadcast_to(primal, (8, 128))
        stats[1] = jnp.broadcast_to((slabs * penalty * penalty) * total(jnp.square(mean)), (8, 128))

    better[...] = polished(better[...])
    collected(gathered, gather_send, gather_recv)
    mean = from_tiles(lambda t: gathered[t // chunk, t % chunk], rows, columns)
    first = local[...]
    c = 2.0 * mean - first
    z = exact(c, phi[...]) * (1.0 / (phi.shape[1] * penalty))
    result = 2.0 * mean - exact(exact(z, better[...]), phi[...], NT)
    to_tiles(result, tiles2)
    end2 = scatter(tiles2, received2, scatter_send2, scatter_recv2)
    after[...] = result

    @pl.when(me < owners)
    def _():
        arrivals(tiles2, received2, scatter_send2, scatter_recv2)
        mine = tiles2[pl.ds(me * chunk, chunk)]
        others = received2[1:slabs]
        old = gathered[me]
        new = (mine + others.sum(0)) * (1.0 / slabs)
        primal = total(jnp.square(mine - new)) + total(jnp.square(others - new[None]))
        dual = (slabs * penalty * penalty) * total(jnp.square(new - old))
        sub = lax.broadcasted_iota(jnp.int32, (8, 128), 0)
        lane = lax.broadcasted_iota(jnp.int32, (8, 128), 1)
        top = jnp.where(lane == 0, stats[0], jnp.broadcast_to(primal, (8, 128)))
        low = jnp.where(lane == 0, stats[1], jnp.broadcast_to(dual, (8, 128)))
        gathered2[me, 0:chunk] = new
        gathered2[me, chunk] = jnp.where(sub == 0, top, low)
        spread(gathered2, gather_send2, gather_recv2)
        for f in range(1, feats):

            def outward(d, f=f):
                copy(
                    gathered2.at[me, chunk], foreign.at[f - 1, me], foreign_send.at[f - 1, d],
                    foreign_recv.at[f - 1, me], peer(d), feat_of(f),
                ).start()

            each(0, slabs, outward)

    collected(gathered2, gather_send2, gather_recv2)
    new = from_tiles(lambda t: gathered2[t // chunk, t % chunk], rows, columns)
    last[...] = new
    change = (first - mean) + (result - new)
    duals[...] = change
    sums = gathered2[0, chunk]
    for o in range(1, owners):
        sums = sums + gathered2[o, chunk]
    for f in range(1, feats):

        def inward(o, f=f):
            copy(
                gathered2.at[0, chunk], foreign.at[f - 1, o], foreign_send.at[f - 1, 0],
                foreign_recv.at[f - 1, o], me, core,
            ).wait_recv()

        each(0, owners, inward)
        for o in range(owners):
            sums = sums + foreign[f - 1, o]
    history[...] = jnp.sqrt(sums * (1.0 / (slabs * reduced * width)))

    each(1, slabs, end1)
    each(1, slabs, end2)

    @pl.when(me < owners)
    def _():
        def leave(d):
            copy(gathered.at[me], gathered.at[me], gather_send.at[d], gather_recv.at[me], peer(d), core).wait_send()
            copy(
                gathered2.at[me], gathered2.at[me], gather_send2.at[d], gather_recv2.at[me], peer(d), core
            ).wait_send()

        each(1, slabs, leave)
        for f in range(1, feats):

            def depart(d, f=f):
                copy(
                    gathered2.at[me, chunk], foreign.at[f - 1, me], foreign_send.at[f - 1, d],
                    foreign_recv.at[f - 1, me], peer(d), feat_of(f),
                ).wait_send()

            each(0, slabs, depart)


def last_kernel(after, duals, last, history, out_after, out_duals, out_last, out_history):
    half, width = out_last.shape
    for r in range(half):
        out_after[r] = after[r : r + 1, :width]
        out_duals[r] = duals[r : r + 1, :width]
    out_last[...] = last[:half, :width]
    out_history[...] = history[0:2, 0:2]


LIMIT = 20 * 2**20


def up(value, step):
    return -(-value // step) * step


def shards(states, inputs, targets):
    reduced = states.shape[0]
    feats = lax.axis_size("feat")
    slabs = lax.axis_size("slab")
    half = reduced // feats
    width = reduced + reduced * (reduced + 1) // 2 + 2
    count = states.shape[1] * feats
    rows, columns = up(half, 8), up(width, 128)
    pieces = (rows // 8) * (columns // 128)
    chunk = -(-pieces // slabs)
    owners = -(-pieces // chunk)
    f32 = jnp.float32
    packed = lax.all_gather(jnp.concatenate([states, targets, inputs[None]], 0), "feat", axis=1, tiled=True)
    vmem = pl.BlockSpec(memory_space=pltpu.VMEM)
    square = jax.ShapeDtypeStruct((count, count), f32)
    system, inverse = pl.pallas_call(
        functools.partial(first_kernel, reduced=reduced),
        out_shape=(square, square),
        in_specs=[vmem],
        out_specs=(vmem,) * 2,
        scratch_shapes=[pltpu.VMEM((count, count), f32)],
        compiler_params=pltpu.CompilerParams(vmem_limit_bytes=LIMIT),
        name="local_inverse",
    )(packed)
    shard = jax.ShapeDtypeStruct((half, width), f32)
    spread_rows = jax.ShapeDtypeStruct((half, 1, width), f32)
    block = jax.ShapeDtypeStruct((rows, columns), f32)
    dma = pltpu.SemaphoreType.DMA
    after, duals, last, history = pl.pallas_call(
        functools.partial(second_kernel, reduced=reduced, width=width),
        out_shape=(block, block, block, jax.ShapeDtypeStruct((8, 128), f32)),
        in_specs=[vmem] * 3,
        out_specs=(vmem,) * 4,
        scratch_shapes=[
            pltpu.VMEM((rows, columns), f32),
            pltpu.VMEM((owners * chunk, 8, 128), f32),
            pltpu.VMEM((columns, count), f32),
            pltpu.VMEM((rows, count), f32),
            pltpu.VMEM((count, count), f32),
            pltpu.VMEM((slabs, chunk, 8, 128), f32),
            pltpu.VMEM((owners, chunk, 8, 128), f32),
            pltpu.VMEM((slabs, chunk, 8, 128), f32),
            pltpu.VMEM((owners, chunk + 1, 8, 128), f32),
            pltpu.VMEM((max(feats - 1, 1), owners, 8, 128), f32),
            pltpu.VMEM((owners * chunk, 8, 128), f32),
            pltpu.VMEM((2, 8, 128), f32),
            dma((slabs,)), dma((slabs,)), dma((slabs,)), dma((owners,)),
            dma((slabs,)), dma((slabs,)), dma((slabs,)), dma((owners,)),
            dma((max(feats - 1, 1), slabs)), dma((max(feats - 1, 1), owners)),
        ],
        compiler_params=pltpu.CompilerParams(vmem_limit_bytes=LIMIT, collective_id=0, has_side_effects=True),
        name="second_and_averages",
    )(packed, system, inverse)
    after, duals, last, history = pl.pallas_call(
        last_kernel,
        out_shape=(spread_rows, spread_rows, shard, jax.ShapeDtypeStruct((2, 2), f32)),
        in_specs=[vmem] * 4,
        out_specs=(vmem,) * 4,
        compiler_params=pltpu.CompilerParams(vmem_limit_bytes=4 * 2**20),
        name="outputs",
    )(after, duals, last, history)
    return (jnp.swapaxes(after, 0, 1), jnp.swapaxes(duals, 0, 1), last, history)


def solution(mesh):
    in_specs = (P(None, ("slab", "feat")), P(("slab", "feat")), P(None, ("slab", "feat")))
    out_specs = (P("slab", "feat", None), P("slab", "feat", None), P("feat", None), P())
    return jax.shard_map(shards, mesh=mesh, in_specs=in_specs, out_specs=out_specs, check_vma=False)
```
